32 devices in a mesh: row: 16 (over z, y, core), col: 2 (over x).
Axes of the slice: x: 2, y: 2, z: 4, core: 2. Of those that a mesh axis runs over, the one named last changes fastest.
Arguments:
- jacobian: bfloat16 [512, 256, 128], P(('col', 'row')), may hold values from -1.5 to 1.5
- weights: bfloat16 [32, 512, 256], P('row', 'col'), may hold values from 0.25 to 4
- panel_weights: bfloat16 [512, 256], P(('col', 'row')), may hold values from 0.25 to 4
- damping: float32 [32, 128], P('row'), may hold values from 0.01 to 1
- panel_inverse: float32 [128, 128], replicated, may hold values from -0.12 to 0.12
Outputs:
- schur: float32 [4096, 65536], P('row', 'col')
The draws below stay inside these ranges and needn't reach their ends.
All inputs are finite; a program needn't handle non-finite values.
Results may differ from the reference program's by a relative error of at most 0.0022.
Values may be sent and summed in bfloat16 or wider, within the bound.
No kernel may reach another device: no remote copies, remote signals or barrier semaphores. Data moves between devices by JAX's collectives and lax.ppermute only.
A program may use at most 128 MiB of HBM per device.

```python
import math
import jax
import jax.numpy as jnp
from jax import lax

NST = 512
PW = 128
ROWS = 256
SLAB = 32


def shard_levels(key, shape, cuts, smallest, largest):
    factor_of, own = 1.0, jax.random.fold_in(key, 6)
    for axis_at, shards_of in cuts:
        draws = jnp.exp(jax.random.uniform(jax.random.fold_in(own, axis_at), (shards_of,), jnp.float32, smallest / len(cuts), largest / len(cuts)))
        factor_of = factor_of * jnp.repeat(draws, shape[axis_at] // shards_of).reshape([-1 if axis == axis_at else 1 for axis in range(len(shape))])
    return factor_of


def gaussian(stream_key, shape, width, most, split=(), kind=jnp.bfloat16):
    values = jax.random.normal(stream_key, shape, jnp.float32) * width
    if len(split) > 0:
        values = shard_levels(stream_key, shape, split, -0.22, 0.18) * values
    return jnp.clip(values, min=-most, max=most).astype(kind)


def setup_inputs(seed: int = 0) -> dict:
    key_of = jax.random.split(jax.random.key(seed), 6)
    return {
        "jacobian": gaussian(key_of[0], (NST, ROWS, PW), 0.25, 1.5, ((0, 32),)),
        "weights": jnp.clip(jnp.exp(math.log(4.0) - 2.7725887 * jax.random.uniform(key_of[1], (SLAB, NST, ROWS), jnp.float32) ** shard_levels(key_of[1], (SLAB, NST, ROWS), ((0, 16), (1, 2)), -0.2, 0.2)), 0.25, 4.0).astype(jnp.bfloat16),
        "panel_weights": jnp.clip(jnp.exp(math.log(4.0) - 2.7725887 * jax.random.uniform(key_of[2], (NST, ROWS), jnp.float32) ** shard_levels(key_of[2], (NST, ROWS), ((0, 32),), -0.2, 0.2)), 0.25, 4.0).astype(jnp.bfloat16),
        "damping": jnp.clip(jnp.exp(math.log(1.0) - 4.6051702 * jax.random.uniform(key_of[3], (SLAB, PW), jnp.float32) ** shard_levels(key_of[3], (SLAB, PW), ((0, 16),), -0.2, 0.2)), 0.01, 1.0),
        "panel_inverse": gaussian(key_of[4], (PW, PW), 0.02, 0.12, (), jnp.float32),
    }


HIGHEST = lax.Precision.HIGHEST


def reference(jacobian, weights, panel_weights, damping, panel_inverse):
    station_count = jacobian.shape[0]
    slab_count = weights.shape[0]
    param_width = jacobian.shape[2]
    panel_id = station_count - 1
    station = jnp.arange(station_count, dtype=jnp.int32)
    jac_float = jacobian.astype(jnp.float32)
    panel_scaled = panel_weights.astype(jnp.float32)[:, :, None] * jac_float
    panel_scaled = jnp.where((station == panel_id)[:, None, None], 0.0, panel_scaled)
    panel_scaled = lax.optimization_barrier(panel_scaled.astype(jnp.bfloat16)).astype(jnp.float32)
    panel_row = jnp.einsum('jra,rb->jab', panel_scaled, jac_float[panel_id])

    def one_row(row_inputs):
        weight_row, jac_row, damp_row, slab_index = row_inputs
        scaled = weight_row.astype(jnp.float32)[:, :, None] * jac_float
        scaled = jnp.where((station == slab_index)[:, None, None], 0.0, scaled)
        scaled = lax.optimization_barrier(scaled.astype(jnp.bfloat16)).astype(jnp.float32)
        coupling = jnp.einsum('jra,rb->ajb', scaled, jac_row.astype(jnp.float32))
        gram_sum = jnp.einsum('jra,jrb->ab', scaled, jac_float)
        diag_block = gram_sum + jnp.diag(jnp.diagonal(gram_sum) * damp_row)
        hessian = jnp.where((station == slab_index)[None, :, None], diag_block[:, None, :], coupling)
        panel_factor = jnp.dot(hessian[:, panel_id, :], panel_inverse, precision=HIGHEST, preferred_element_type=jnp.float32)
        correction = jnp.einsum('ac,jcb->ajb', panel_factor, panel_row, precision=HIGHEST)
        schur = jnp.where((station == panel_id)[None, :, None], panel_factor[:, None, :], hessian - correction)
        return schur.reshape(param_width, station_count * param_width)

    result = lax.map(one_row, (weights, jacobian[:slab_count], damping, jnp.arange(slab_count, dtype=jnp.int32)))
    return result.reshape(slab_count * param_width, station_count * param_width)
```

```python
import functools

import jax
import jax.numpy as jnp
import numpy as np
from jax import lax
from jax.experimental import pallas as pl
from jax.experimental.pallas import tpu as pltpu
from jax.sharding import PartitionSpec as P

HIGHEST = lax.Precision.HIGHEST
F32 = jnp.float32
BF16 = jnp.bfloat16


def dot_nt(a, b):
    return lax.dot_general(a, b, (((1,), (1,)), ((), ())), preferred_element_type=F32)


def block_kernel(slot, group, has_out, sc, jac, w, pw, slab_t, panel_t, fac, fac_b, gin, *refs):
    out, gout = refs[-2:]
    slabs, width, _ = slab_t.shape
    extra = sc.shape[0] - slabs - 1
    step = pl.program_id(0)
    first = sc[slot] + step * group
    acc = None
    blocks, panels = [], []
    for k in range(group):
        j = first + k
        jac_t = jac[k].T
        rows = [
            jnp.where(j == sc[extra + 1 + i], 0.0, w[i, pl.ds(j, 1), :]).astype(BF16)
            for i in range(slabs)
        ]
        row_p = pw[pl.ds(j, 1), :].astype(BF16)
        blocks.append(
            dot_nt(jac_t, jnp.concatenate([slab_t[i] * rows[i] for i in range(slabs)], 0))
        )
        panels.append(dot_nt(jac_t, panel_t[...] * row_p).astype(BF16))
        part = dot_nt(jac_t, jnp.concatenate([jac_t * rows[i] for i in range(slabs)], 0))
        acc = part if acc is None else acc + part
    corr = jnp.dot(fac_b[...], jnp.concatenate(panels, 1), preferred_element_type=F32)
    for k in range(group):
        for i in range(slabs):
            here = (slice(i * width, (i + 1) * width), slice(k * width, (k + 1) * width))
            out[here] = blocks[k][:, i * width : (i + 1) * width] - corr[here]

    @pl.when(step == 0)
    def _():
        gout[...] = gin[...] + acc

    @pl.when(step != 0)
    def _():
        gout[...] += acc

    where_p = sc[extra] - first
    for k in range(group):

        @pl.when(where_p == k)
        def _():
            out[:, k * width : (k + 1) * width] = fac[...]


def block_call(slot, sc, jac, w, pw, slab_t, panel_t, fac, fac_b, gram, out, shape):
    count, rows, width = jac.shape
    slabs = slab_t.shape[0]
    group = next(g for g in (8, 4, 2, 1) if count % g == 0)

    def full(a):
        return pl.BlockSpec(a.shape, lambda g, s: (0,) * a.ndim)

    args = [jac, w, pw, slab_t, panel_t, fac, fac_b, gram]
    specs = [pl.BlockSpec((group, rows, width), lambda g, s: (g, 0, 0))]
    specs += [full(a) for a in args[1:]]
    aliases = {8: 1}
    if out is not None:
        args.append(out)
        specs.append(pl.BlockSpec(memory_space=pl.ANY))
        aliases[9] = 0
    return pl.pallas_call(
        functools.partial(block_kernel, slot, group, out is not None),
        grid_spec=pltpu.PrefetchScalarGridSpec(
            num_scalar_prefetch=1,
            grid=(count // group,),
            in_specs=specs,
            out_specs=[
                pl.BlockSpec((slabs * width, group * width), lambda g, s: (0, s[slot] // group + g)),
                full(gram),
            ],
        ),
        out_shape=[
            jax.ShapeDtypeStruct(shape, F32),
            jax.ShapeDtypeStruct(gram.shape, F32),
        ],
        input_output_aliases=aliases,
        compiler_params=pltpu.CompilerParams(vmem_limit_bytes=40 << 20),
        cost_estimate=pl.CostEstimate(
            flops=count * 14 * width * width * rows,
            bytes_accessed=count * slabs * width * width * 4 + count * rows * width * 2,
            transcendentals=0,
        ),
    )(sc, *args)


def patch_kernel(sc, gram, damp, tile, out):
    i = pl.program_id(0)
    width = tile.shape[0]
    g = gram[...].T
    eye = lax.broadcasted_iota(jnp.int32, (width, width), 0) == lax.broadcasted_iota(
        jnp.int32, (width, width), 1
    )
    full = jnp.where(eye, g * (1.0 + damp[pl.ds(i, 1), :]), g)
    out[...] = jnp.where(sc[2 * i + 1] > 0, tile[...] + full, tile[...])


def patch_call(sc, gram, damping, out):
    slabs, width = damping.shape
    tile = pl.BlockSpec((width, width), lambda i, s: (i, s[2 * i]))
    return pl.pallas_call(
        patch_kernel,
        grid_spec=pltpu.PrefetchScalarGridSpec(
            num_scalar_prefetch=1,
            grid=(slabs,),
            in_specs=[
                pl.BlockSpec((width, width), lambda i, s: (0, i)),
                pl.BlockSpec((slabs, width), lambda i, s: (0, 0)),
                tile,
            ],
            out_specs=tile,
        ),
        out_shape=jax.ShapeDtypeStruct(out.shape, F32),
        input_output_aliases={3: 0},
    )(sc, gram, damping, out)


def chip_cycle(chips, cols):
    if cols == 2:
        return list(range(0, chips, 2)) + list(range(chips - 1, 0, -2))
    half = chips // 2
    return list(range(half)) + list(range(chips - 1, half - 1, -1))


def shards(jacobian, weights, panel_weights, damping, panel_inverse):
    per_dev, samples, width = jacobian.shape
    slabs, col_block, _ = weights.shape
    rows = lax.axis_size("row")
    cols = lax.axis_size("col")
    row = lax.axis_index("row")
    col = lax.axis_index("col")
    panel_id = col_block * cols - 1

    chips = rows // 2
    cycle = chip_cycle(chips, cols)
    place = {c: p for p, c in enumerate(cycle)}
    ahead = [(2 * c + k, 2 * cycle[(place[c] + 1) % chips] + k) for c in cycle for k in (0, 1)]
    back = [(t, s) for s, t in ahead]
    swap = [(r, r ^ 1) for r in range(rows)]
    half = per_dev // 2

    pw_all = lax.all_gather(panel_weights, "row", axis=0, tiled=True).astype(F32)
    holds_panel = (row == rows - 1) & (col == cols - 1)
    panel_jac = lax.psum(
        jnp.where(holds_panel, jacobian[per_dev - 1], jnp.zeros_like(jacobian[0])), ("row", "col")
    )
    w_panel = lax.psum(
        jnp.where(col == cols - 1, weights[:, col_block - 1], jnp.zeros_like(weights[:, 0])), "col"
    )
    slab = jnp.zeros((slabs, samples, width), BF16)
    for offset in range(0, per_dev, slabs):
        piece = lax.slice_in_dim(jacobian, offset, offset + slabs, axis=0)
        pairs = []
        for t in range(rows):
            if (t * slabs) % per_dev == offset:
                home = (t * slabs) // per_dev
                source, target = (home % rows) * cols + home // rows, t * cols
                if source == target:
                    slab = slab + jnp.where((row == t) & (col == 0), piece, jnp.zeros_like(piece))
                else:
                    pairs.append((source, target))
        if pairs:
            slab = slab + lax.ppermute(piece, ("row", "col"), pairs)
    spread = slab
    for c in range(1, cols):
        spread = spread + lax.ppermute(slab, "col", [(0, c)])
    slab = spread

    scaled_p = (w_panel.astype(F32)[:, :, None] * panel_jac.astype(F32)[None]).astype(BF16)
    hess_p = jnp.einsum("ira,irb->iab", scaled_p, slab, preferred_element_type=F32)
    factor = jnp.einsum(
        "iac,cb->iab", hess_p, panel_inverse, precision=HIGHEST, preferred_element_type=F32
    ).reshape(slabs * width, width)
    factor_b = factor.astype(BF16)
    slab_t = jnp.swapaxes(slab, 1, 2)
    panel_t = panel_jac.T
    w32 = weights.astype(F32)

    pieces = []
    lo, hi = jacobian[:half], jacobian[half:]
    pieces.append((jacobian, 0, 0, 0))
    pieces.append((lax.ppermute(jacobian, "row", swap), 0, 1, 0))
    fwd, bwd = [lo, hi], [lo, hi]
    for d in range(1, chips // 2 + 1):
        last = d == chips // 2
        for k in (0, 1):
            if not last or k == 0:
                fwd[k] = lax.ppermute(fwd[k], "row", ahead)
                pieces.append((fwd[k], -d, 0, k))
                pieces.append((lax.ppermute(fwd[k], "row", swap), -d, 1, k))
            if not last or k == 1:
                bwd[k] = lax.ppermute(bwd[k], "row", back)
                pieces.append((bwd[k], d, 0, k))
                pieces.append((lax.ppermute(bwd[k], "row", swap), d, 1, k))

    table = np.zeros((rows, len(pieces)), np.int32)
    for r in range(rows):
        for n, (_, d, other, k) in enumerate(pieces):
            chip = cycle[(place[r // 2] + d) % chips]
            table[r, n] = (2 * chip + ((r % 2) ^ other)) * per_dev + k * half
    starts = lax.dynamic_index_in_dim(jnp.asarray(table), row, 0, keepdims=False)
    base = col * col_block
    ids = row * slabs + jnp.arange(slabs, dtype=jnp.int32) - base
    sc = jnp.concatenate([starts, (panel_id - base)[None].astype(jnp.int32), ids])

    shape = (slabs * width, col_block * width)
    gram = jnp.zeros((width, slabs * width), F32)
    out = None
    for n, (value, _, _, _) in enumerate(pieces):
        out, gram = block_call(
            n, sc, value, w32, pw_all, slab_t, panel_t, factor, factor_b, gram, out, shape
        )
    if cols == 2:
        gram = gram + lax.ppermute(gram, "col", [(0, 1), (1, 0)])
    else:
        gram = lax.psum(gram, "col")
    held = ((ids >= 0) & (ids < col_block)).astype(jnp.int32)
    patch = jnp.stack([jnp.clip(ids, 0, col_block - 1), held], 1).reshape(-1)
    return patch_call(patch, gram, damping, out)


def solution(mesh):
    return jax.shard_map(
        shards,
        mesh=mesh,
        in_specs=(
            P(("col", "row"), None, None),
            P("row", "col", None),
            P(("col", "row"), None),
            P("row", None),
            P(),
        ),
        out_specs=P("row", "col"),
        check_vma=False,
    )
```

```python
import functools

import jax
import jax.numpy as jnp
import numpy as np
from jax import lax
from jax.experimental import pallas as pl
from jax.experimental.pallas import tpu as pltpu
from jax.sharding import PartitionSpec as P

HIGHEST = lax.Precision.HIGHEST
F32 = jnp.float32
BF16 = jnp.bfloat16


def dot_nt(a, b):
    return lax.dot_general(a, b, (((1,), (1,)), ((), ())), preferred_element_type=F32)


def prep_kernel(slab, panel, w_panel, inverse, slab_t, panel_t, fac, fac_b):
    width = panel.shape[1]
    p_t = panel[...].T
    panel_t[...] = p_t
    for i in range(slab.shape[0]):
        s = slab[i]
        slab_t[i] = s.T
        scaled = p_t * w_panel[pl.ds(i, 1), :].astype(BF16)
        hess = jnp.dot(scaled, s, preferred_element_type=F32)
        f = jnp.dot(hess, inverse[...], precision=HIGHEST, preferred_element_type=F32)
        fac[i * width : (i + 1) * width] = f
        fac_b[i * width : (i + 1) * width] = f.astype(BF16)


def prep_call(slab, panel, w_panel, inverse):
    slabs, rows, width = slab.shape
    return pl.pallas_call(
        prep_kernel,
        out_shape=[
            jax.ShapeDtypeStruct((slabs, width, rows), BF16),
            jax.ShapeDtypeStruct((width, rows), BF16),
            jax.ShapeDtypeStruct((slabs * width, width), F32),
            jax.ShapeDtypeStruct((slabs * width, width), BF16),
        ],
    )(slab, panel, w_panel, inverse)


def block_kernel(slot, half, count, skip, sc, w, slab_t, panel_t, fac, fac_b, gin, *refs):
    blocks = refs[:count]
    out, gout, token, jbuf, obuf, in_sem, out_sem = refs[count + skip :]
    token[...] = jnp.zeros_like(token)
    slabs, width, rows = slab_t.shape
    extra = sc.shape[0] - slabs - 1
    for b in range(count):
        pltpu.make_async_copy(blocks[b], jbuf.at[b], in_sem.at[b]).start()
    gout[...] = gin[...]

    def write(b):
        col = pl.multiple_of(sc[slot + b] * width, half * width)
        return pltpu.make_async_copy(
            obuf.at[b % 2], out.at[:, pl.ds(col, half * width)], out_sem.at[b % 2]
        )

    def one(b, carry):
        pltpu.make_async_copy(blocks[0], jbuf.at[b], in_sem.at[b]).wait()

        @pl.when(b >= 2)
        def _():
            write(b - 2).wait()

        first = sc[slot + b]
        pw = jbuf[b, half * rows : half * rows + 2 * half, :].astype(F32)
        acc = None
        parts, panels = [], []
        for k in range(half):
            j = first + k
            jac_t = jbuf[b, k * rows : (k + 1) * rows, :].T
            ws = [
                jnp.where(j == sc[extra + 1 + i], 0.0, w[i, pl.ds(j, 1), :]).astype(BF16)
                for i in range(slabs)
            ]
            row_p = jnp.concatenate([pw[k : k + 1], pw[half + k : half + k + 1]], 1).astype(BF16)
            parts.append(
                dot_nt(jac_t, jnp.concatenate([slab_t[i] * ws[i] for i in range(slabs)], 0))
            )
            panels.append(dot_nt(jac_t, panel_t[...] * row_p).astype(BF16))
            part = dot_nt(jac_t, jnp.concatenate([jac_t * ws[i] for i in range(slabs)], 0))
            acc = part if acc is None else acc + part
        corr = jnp.dot(fac_b[...], jnp.concatenate(panels, 1), preferred_element_type=F32)
        o = obuf.at[b % 2]
        for k in range(half):
            for i in range(slabs):
                here = (slice(i * width, (i + 1) * width), slice(k * width, (k + 1) * width))
                o[here] = parts[k][:, i * width : (i + 1) * width] - corr[here]
        gout[...] += acc
        where_p = sc[extra] - first

        @pl.when((where_p >= 0) & (where_p < half))
        def _():
            for k in range(half):

                @pl.when(where_p == k)
                def _():
                    o[:, k * width : (k + 1) * width] = fac[...]

        write(b).start()
        return carry

    lax.fori_loop(0, count, one, 0)
    for b in range(max(count - 2, 0), count):
        write(b).wait()


def block_call(slot, half, sc, blocks, w, slab_t, panel_t, fac, fac_b, gram, after, out, shape):
    slabs, width, rows = slab_t.shape
    count = len(blocks)
    args = [w, slab_t, panel_t, fac, fac_b, gram] + list(blocks) + list(after)
    specs = [pl.BlockSpec(memory_space=pltpu.VMEM)] * 6
    specs += [pl.BlockSpec(memory_space=pltpu.HBM)] * count
    specs += [pl.BlockSpec(memory_space=pl.ANY)] * len(after)
    aliases = {6: 1}
    if out is not None:
        aliases[1 + len(args)] = 0
        args.append(out)
        specs.append(pl.BlockSpec(memory_space=pl.ANY))
    stations = half * count
    return pl.pallas_call(
        functools.partial(
            block_kernel, slot, half, count, len(after) + (out is not None)
        ),
        in_specs=[pl.BlockSpec(memory_space=pltpu.SMEM)] + specs,
        out_specs=[pl.BlockSpec(memory_space=pl.ANY)] + [pl.BlockSpec(memory_space=pltpu.VMEM)] * 2,
        out_shape=[
            jax.ShapeDtypeStruct(shape, F32),
            jax.ShapeDtypeStruct(gram.shape, F32),
            jax.ShapeDtypeStruct((8, 128), F32),
        ],
        scratch_shapes=[
            pltpu.VMEM((count,) + blocks[0].shape, BF16),
            pltpu.VMEM((2, slabs * width, half * width), F32),
            pltpu.SemaphoreType.DMA((count,)),
            pltpu.SemaphoreType.DMA((2,)),
        ],
        input_output_aliases=aliases,
        compiler_params=pltpu.CompilerParams(vmem_limit_bytes=24 << 20),
        cost_estimate=pl.CostEstimate(
            flops=stations * 14 * width * width * rows,
            bytes_accessed=stations * (slabs * width * width * 4 + rows * width * 2),
            transcendentals=0,
        ),
    )(sc, *args)


def patch_kernel(sc, gram, other, damp, tile, out):
    i = pl.program_id(0)
    width = tile.shape[0]
    g = (gram[...] + other[...]).T
    eye = lax.broadcasted_iota(jnp.int32, (width, width), 0) == lax.broadcasted_iota(
        jnp.int32, (width, width), 1
    )
    full = jnp.where(eye, g * (1.0 + damp[pl.ds(i, 1), :]), g)
    out[...] = jnp.where(sc[2 * i + 1] > 0, tile[...] + full, tile[...])


def patch_call(sc, gram, other, damping, out):
    slabs, width = damping.shape
    tile = pl.BlockSpec((width, width), lambda i, s: (i, s[2 * i]))
    part = pl.BlockSpec((width, width), lambda i, s: (0, i))
    return pl.pallas_call(
        patch_kernel,
        grid_spec=pltpu.PrefetchScalarGridSpec(
            num_scalar_prefetch=1,
            grid=(slabs,),
            in_specs=[part, part, pl.BlockSpec((slabs, width), lambda i, s: (0, 0)), tile],
            out_specs=tile,
        ),
        out_shape=jax.ShapeDtypeStruct(out.shape, F32),
        input_output_aliases={4: 0},
    )(sc, gram, other, damping, out)


def chip_cycle(chips, cols):
    if cols == 2:
        return list(range(0, chips, 2)) + list(range(chips - 1, 0, -2))
    half = chips // 2
    return list(range(half)) + list(range(chips - 1, half - 1, -1))


def spread_direct(jacobian, weights, row, col):
    per_dev, samples, width = jacobian.shape
    slabs = weights.shape[0]
    core, y = row % 2, (row // 2) % 2
    both = ("row", "col")
    w_mine = weights[:, -1].reshape(slabs * samples // width, width)
    w_mine = jnp.pad(w_mine, ((0, samples - w_mine.shape[0]), (0, 0)))
    quads = 2 * slabs
    ends = [None, (11, 1), (7, 1), (3, 1)]
    is_panel = col == 1
    mine = jacobian[per_dev - 1]
    panel_pay = jnp.concatenate([mine[None]] + [jnp.zeros_like(jacobian[: quads - 1])], 0)
    total = jnp.where((row == 15) & is_panel, panel_pay, jnp.zeros_like(panel_pay))
    total = total + jnp.where((row == 0) & (col == 0), jacobian[:quads], jnp.zeros_like(panel_pay))
    for m in (1, 2, 3, 0):
        pay = jnp.where(is_panel, panel_pay, lax.slice_in_dim(jacobian, quads * m, quads * (m + 1)))
        pairs = [(2, 2 * (8 + 2 * m))]
        if m:
            pairs += [(0, 4 * m), (31, 2 * ends[m][0] + ends[m][1])]
        total = total + lax.ppermute(pay, both, pairs)
    hop = [(2 * r, 2 * (r ^ 1)) for r in range(16)] + [(2 * r + 1, 2 * (r ^ 2) + 1) for r in range(16)]
    first = lax.ppermute(jnp.where(is_panel, total[:slabs], total[slabs:]), both, hop)
    slab = jnp.where(core == 0, total[:slabs], first)
    panel = jnp.where(y == 1, total[0], first[0])
    far = jnp.stack([panel, w_mine], 0)
    second = lax.ppermute(jnp.where(is_panel, far, slab), "col", [(0, 1), (1, 0)])
    slab = jnp.where(is_panel, second, slab)
    far = jnp.where(is_panel, far, second)
    third = lax.ppermute(far[0], "row", [(r, r ^ 1) for r in range(16)])
    panel = jnp.where(core == 1, far[0], third)
    w_panel = far[1][: slabs * samples // width].reshape(slabs, samples)
    return slab, panel, w_panel


def spread_general(jacobian, weights, row, col, rows, cols):
    per_dev, samples, width = jacobian.shape
    slabs = weights.shape[0]
    holds = (row == rows - 1) & (col == cols - 1)
    panel = lax.psum(
        jnp.where(holds, jacobian[per_dev - 1], jnp.zeros_like(jacobian[0])), ("row", "col")
    )
    w_panel = lax.psum(
        jnp.where(col == cols - 1, weights[:, -1], jnp.zeros_like(weights[:, 0])), "col"
    )
    slab = jnp.zeros((slabs, samples, width), BF16)
    for offset in range(0, per_dev, slabs):
        piece = lax.slice_in_dim(jacobian, offset, offset + slabs, axis=0)
        pairs = []
        for t in range(rows):
            if (t * slabs) % per_dev == offset:
                home = (t * slabs) // per_dev
                source, target = (home % rows) * cols + home // rows, t * cols
                if source == target:
                    slab = slab + jnp.where((row == t) & (col == 0), piece, jnp.zeros_like(piece))
                else:
                    pairs.append((source, target))
        if pairs:
            slab = slab + lax.ppermute(piece, ("row", "col"), pairs)
    spread = slab
    for c in range(1, cols):
        spread = spread + lax.ppermute(slab, "col", [(0, c)])
    return spread, panel, w_panel


def shards(jacobian, weights, panel_weights, damping, panel_inverse):
    per_dev, samples, width = jacobian.shape
    slabs, col_block, _ = weights.shape
    rows = lax.axis_size("row")
    cols = lax.axis_size("col")
    row = lax.axis_index("row")
    col = lax.axis_index("col")
    panel_id = col_block * cols - 1

    chips = rows // 2
    cycle = chip_cycle(chips, cols)
    place = {c: p for p, c in enumerate(cycle)}
    ahead = [(2 * c + k, 2 * cycle[(place[c] + 1) % chips] + k) for c in cycle for k in (0, 1)]
    back = [(t, s) for s, t in ahead]
    swap = [(r, r ^ 1) for r in range(rows)]
    half = per_dev // 2

    if (rows, cols, per_dev) == (16, 2, 8 * slabs):
        slab, panel_jac, w_panel = spread_direct(jacobian, weights, row, col)
    else:
        slab, panel_jac, w_panel = spread_general(jacobian, weights, row, col, rows, cols)
    slab_t, panel_t, factor, factor_b = prep_call(
        slab, panel_jac, w_panel.astype(F32), panel_inverse
    )
    w32 = weights.astype(F32)

    def pack(k):
        own = slice(k * half, (k + 1) * half)
        p = panel_weights[own]
        tail = jnp.concatenate([p[:, :width], p[:, width:]], 0)
        tail = jnp.pad(tail, ((0, -tail.shape[0] % 16), (0, 0)))
        return jnp.concatenate([jacobian[own].reshape(half * samples, width), tail], 0)

    def over(value, perm):
        return lax.ppermute(value, "row", perm)

    own = [pack(0), pack(1)]
    tokens, after = [], []
    gram = jnp.zeros((width, slabs * width), F32)
    shape = (slabs * width, col_block * width)
    out = None
    plan = []

    def compute(call):
        nonlocal out, gram
        slot = len(plan)
        plan.extend(p[1:] for p in call)
        out, gram, token = block_call(
            slot, half, sc, [p[0] for p in call],
            w32, slab_t, panel_t, factor, factor_b, gram, tuple(after), out, shape,
        )
        after.clear()
        tokens.append(token)

    order = [(0, 0, 0), (0, 0, 1), (0, 1, 0), (0, 1, 1)]
    far = chips // 2
    for d in range(1, far):
        for k in (0, 1):
            order += [(-d, 0, k), (d, 0, k), (-d, 1, k), (d, 1, k)]
    order += [(-far, 0, 0), (far, 0, 1), (-far, 1, 0), (far, 1, 1)]
    table = np.zeros((rows, len(order)), np.int32)
    for r in range(rows):
        for n, (dist, other, k) in enumerate(order):
            chip = cycle[(place[r // 2] + dist) % chips]
            table[r, n] = (2 * chip + ((r % 2) ^ other)) * per_dev + k * half
    starts = lax.dynamic_index_in_dim(jnp.asarray(table), row, 0, keepdims=False)
    base = col * col_block
    ids = row * slabs + jnp.arange(slabs, dtype=jnp.int32) - base
    sc = jnp.concatenate([starts, (panel_id - base)[None].astype(jnp.int32), ids])
    held = ((ids >= 0) & (ids < col_block)).astype(jnp.int32)
    spots = jnp.stack([jnp.clip(ids, 0, col_block - 1), held], 1).reshape(-1)

    hops = [(over(own[k], ahead), over(own[k], back)) for k in (0, 1)]
    compute(
        [(own[0], 0, 0, 0), (own[1], 0, 0, 1)] + [(over(own[k], swap), 0, 1, k) for k in (0, 1)]
    )
    for q in range(2 * (far - 1)):
        d, k = q // 2 + 1, q % 2
        f, b = hops[q]
        if q == 1:
            f, b, factor_b = lax.optimization_barrier((f, b, factor_b))
        elif q > 1:
            f, b, ready = lax.optimization_barrier((f, b, tokens[q - 1]))
            after.append(ready)
        if d + 1 < far:
            hops.append((over(f, ahead), over(b, back)))
        elif k == 0:
            last_f = over(f, ahead)
        else:
            last_b = over(b, back)
        compute([(f, -d, 0, k), (b, d, 0, k), (over(f, swap), -d, 1, k), (over(b, swap), d, 1, k)])
    compute([(last_f, -far, 0, 0), (last_b, far, 0, 1)])
    compute([(over(last_f, swap), -far, 1, 0), (over(last_b, swap), far, 1, 1)])
    assert plan == order
    if cols == 2:
        other = lax.ppermute(gram, "col", [(0, 1), (1, 0)])
    else:
        other = lax.psum(gram, "col") - gram
    return patch_call(spots, gram, other, damping, out)


def solution(mesh):
    return jax.shard_map(
        shards,
        mesh=mesh,
        in_specs=(
            P(("col", "row"), None, None),
            P("row", "col", None),
            P(("col", "row"), None),
            P("row", None),
            P(),
        ),
        out_specs=P("row", "col"),
        check_vma=False,
    )
```

```python
import functools

import jax
import jax.numpy as jnp
import numpy as np
from jax import lax
from jax.experimental import pallas as pl
from jax.experimental.pallas import tpu as pltpu
from jax.sharding import PartitionSpec as P

HIGHEST = lax.Precision.HIGHEST
F32 = jnp.float32
BF16 = jnp.bfloat16


def dot_nt(a, b):
    return lax.dot_general(a, b, (((1,), (1,)), ((), ())), preferred_element_type=F32)


def prep_kernel(pick, slab_a, slab_b, panel_a, panel_b, w_a, w_b, inverse, *outs):
    turned, fac = outs
    slabs, rows, width = slab_a.shape
    lanes = rows // width
    panel = jnp.where(pick[1] > 0, panel_a[...], panel_b[...])
    w = jnp.where(pick[2] > 0, w_a[...], w_b[...]).astype(F32)
    p_t = panel.T
    turned[slabs] = p_t
    for i in range(slabs):
        s = jnp.where(pick[0] > 0, slab_a[i], slab_b[i])
        turned[i] = s.T
        row = jnp.concatenate([w[i * lanes + n : i * lanes + n + 1] for n in range(lanes)], 1)
        scaled = p_t * row.astype(BF16)
        hess = jnp.dot(scaled, s, preferred_element_type=F32)
        fac[i * width : (i + 1) * width] = jnp.dot(
            hess, inverse[...], precision=HIGHEST, preferred_element_type=F32
        )


def prep_call(pick, slab_a, slab_b, panel_a, panel_b, w_a, w_b, inverse):
    slabs, rows, width = slab_a.shape
    return pl.pallas_call(
        prep_kernel,
        in_specs=[pl.BlockSpec(memory_space=pltpu.SMEM)]
        + [pl.BlockSpec(memory_space=pltpu.VMEM)] * 7,
        out_specs=[pl.BlockSpec(memory_space=pltpu.VMEM)] * 2,
        out_shape=[
            jax.ShapeDtypeStruct((slabs + 1, width, rows), BF16),
            jax.ShapeDtypeStruct((slabs * width, width), F32),
        ],
    )(pick, slab_a, slab_b, panel_a, panel_b, w_a, w_b, inverse)


def block_kernel(slot, half, count, skip, sc, w, turned, fac, gin, *refs):
    units = refs[: count // 2]
    out, gout, token, jbuf, pbuf, obuf, in_sem, out_sem = refs[count // 2 + skip :]
    slabs = w.shape[0]
    _, width, rows = turned.shape
    extra = sc.shape[0] - slabs - 1
    size, tail = half * rows, pbuf.shape[1]

    def fetch(b):
        unit, h = units[b // 2], b % 2
        return (
            pltpu.make_async_copy(unit.at[pl.ds(h * size, size)], jbuf.at[b], in_sem.at[0, b]),
            pltpu.make_async_copy(
                unit.at[pl.ds(2 * size + h * tail, tail)], pbuf.at[b], in_sem.at[1, b]
            ),
        )

    for b in range(count):
        for copy in fetch(b):
            copy.start()
    token[...] = jnp.zeros_like(token)
    gout[...] = gin[...]
    fac_b = fac[...].astype(BF16)

    def write(b):
        col = pl.multiple_of(sc[slot + b] * width, half * width)
        return pltpu.make_async_copy(
            obuf.at[b % 2], out.at[:, pl.ds(col, half * width)], out_sem.at[b % 2]
        )

    def one(b, carry):
        pltpu.make_async_copy(units[0].at[pl.ds(0, size)], jbuf.at[b], in_sem.at[0, b]).wait()
        pltpu.make_async_copy(units[0].at[pl.ds(0, tail)], pbuf.at[b], in_sem.at[1, b]).wait()

        @pl.when(b >= 2)
        def _():
            write(b - 2).wait()

        first = sc[slot + b]
        pw = pbuf[b].astype(F32)
        acc = None
        parts, panels = [], []
        for k in range(half):
            j = first + k
            jac_t = jbuf[b, k * rows : (k + 1) * rows, :].T
            ws = [
                jnp.where(j == sc[extra + 1 + i], 0.0, w[i, pl.ds(j, 1), :]).astype(BF16)
                for i in range(slabs)
            ]
            row_p = jnp.concatenate([pw[k : k + 1], pw[half + k : half + k + 1]], 1).astype(BF16)
            parts.append(
                dot_nt(jac_t, jnp.concatenate([turned[i] * ws[i] for i in range(slabs)], 0))
            )
            panels.append(dot_nt(jac_t, turned[slabs] * row_p).astype(BF16))
            part = dot_nt(jac_t, jnp.concatenate([jac_t * ws[i] for i in range(slabs)], 0))
            acc = part if acc is None else acc + part
        corr = jnp.dot(fac_b, jnp.concatenate(panels, 1), preferred_element_type=F32)
        o = obuf.at[b % 2]
        for k in range(half):
            for i in range(slabs):
                here = (slice(i * width, (i + 1) * width), slice(k * width, (k + 1) * width))
                o[here] = parts[k][:, i * width : (i + 1) * width] - corr[here]
        gout[...] += acc
        where_p = sc[extra] - first

        @pl.when((where_p >= 0) & (where_p < half))
        def _():
            for k in range(half):

                @pl.when(where_p == k)
                def _():
                    o[:, k * width : (k + 1) * width] = fac[...]

        write(b).start()
        return carry

    lax.fori_loop(0, count, one, 0)
    for b in range(max(count - 2, 0), count):
        write(b).wait()


def block_call(slot, half, sc, units, w, turned, fac, gram, after, out, shape):
    slabs = w.shape[0]
    _, width, rows = turned.shape
    count = 2 * len(units)
    args = [w, turned, fac, gram] + list(units) + list(after)
    specs = [pl.BlockSpec(memory_space=pltpu.VMEM)] * 4
    specs += [pl.BlockSpec(memory_space=pltpu.HBM)] * len(units)
    specs += [pl.BlockSpec(memory_space=pl.ANY)] * len(after)
    aliases = {4: 1}
    if out is not None:
        aliases[1 + len(args)] = 0
        args.append(out)
        specs.append(pl.BlockSpec(memory_space=pl.ANY))
    stations = half * count
    tail = units[0].shape[0] // 2 - half * rows
    return pl.pallas_call(
        functools.partial(block_kernel, slot, half, count, len(after) + (out is not None)),
        in_specs=[pl.BlockSpec(memory_space=pltpu.SMEM)] + specs,
        out_specs=[pl.BlockSpec(memory_space=pl.ANY)] + [pl.BlockSpec(memory_space=pltpu.VMEM)] * 2,
        out_shape=[
            jax.ShapeDtypeStruct(shape, F32),
            jax.ShapeDtypeStruct(gram.shape, F32),
            jax.ShapeDtypeStruct((8, 128), F32),
        ],
        scratch_shapes=[
            pltpu.VMEM((count, half * rows, width), BF16),
            pltpu.VMEM((count, tail, width), BF16),
            pltpu.VMEM((2, slabs * width, half * width), F32),
            pltpu.SemaphoreType.DMA((2, count)),
            pltpu.SemaphoreType.DMA((2,)),
        ],
        input_output_aliases=aliases,
        compiler_params=pltpu.CompilerParams(vmem_limit_bytes=24 << 20),
        cost_estimate=pl.CostEstimate(
            flops=stations * 14 * width * width * rows,
            bytes_accessed=stations * (slabs * width * width * 4 + rows * width * 2),
            transcendentals=0,
        ),
    )(sc, *args)


def patch_kernel(sc, gram, other, damp, tile, out):
    i = pl.program_id(0)
    width = tile.shape[0]
    g = (gram[...] + other[...]).T
    eye = lax.broadcasted_iota(jnp.int32, (width, width), 0) == lax.broadcasted_iota(
        jnp.int32, (width, width), 1
    )
    full = jnp.where(eye, g * (1.0 + damp[pl.ds(i, 1), :]), g)
    out[...] = jnp.where(sc[2 * i + 1] > 0, tile[...] + full, tile[...])


def patch_call(sc, gram, other, damping, out):
    slabs, width = damping.shape
    tile = pl.BlockSpec((width, width), lambda i, s: (i, s[2 * i]))
    part = pl.BlockSpec((width, width), lambda i, s: (0, i))
    return pl.pallas_call(
        patch_kernel,
        grid_spec=pltpu.PrefetchScalarGridSpec(
            num_scalar_prefetch=1,
            grid=(slabs,),
            in_specs=[part, part, pl.BlockSpec((slabs, width), lambda i, s: (0, 0)), tile],
            out_specs=tile,
        ),
        out_shape=jax.ShapeDtypeStruct(out.shape, F32),
        input_output_aliases={4: 0},
    )(sc, gram, other, damping, out)


def chip_cycle(chips, cols):
    if cols == 2:
        return list(range(0, chips, 2)) + list(range(chips - 1, 0, -2))
    half = chips // 2
    return list(range(half)) + list(range(chips - 1, half - 1, -1))


def spread_direct(jacobian, weights, row, col, later):
    per_dev, samples, width = jacobian.shape
    slabs = weights.shape[0]
    core, y = row % 2, (row // 2) % 2
    both = ("row", "col")
    w_mine = weights[:, -1].reshape(slabs * samples // width, width)
    w_mine = jnp.pad(w_mine, ((0, 16 - w_mine.shape[0]), (0, 0)))
    quads = 2 * slabs
    ends = [None, (11, 1), (7, 1), (3, 1)]
    is_panel = col == 1
    mine = jacobian[per_dev - 1]
    panel_pay = jnp.concatenate([mine[None]] + [jnp.zeros_like(jacobian[: quads - 1])], 0)
    total = jnp.where((row == 15) & is_panel, panel_pay, jnp.zeros_like(panel_pay))
    total = total + jnp.where((row == 0) & (col == 0), jacobian[:quads], jnp.zeros_like(panel_pay))
    for m in (1, 2, 3, 0):
        pay = jnp.where(is_panel, panel_pay, lax.slice_in_dim(jacobian, quads * m, quads * (m + 1)))
        pairs = [(2, 2 * (8 + 2 * m))]
        if m:
            pairs += [(0, 4 * m), (31, 2 * ends[m][0] + ends[m][1])]
        total = total + lax.ppermute(pay, both, pairs)
    hop = [(2 * r, 2 * (r ^ 1)) for r in range(16)] + [(2 * r + 1, 2 * (r ^ 2) + 1) for r in range(16)]
    total, later = lax.optimization_barrier((total, later))
    first = lax.ppermute(jnp.where(is_panel, total[:slabs], total[slabs:]), both, hop)
    panel = jnp.where(y == 1, total[0], first[0])
    w_rest = jnp.pad(w_mine, ((0, samples - 16), (0, 0)))
    mixed = jnp.where(core == 0, total[:slabs], first)
    send = jnp.where(is_panel, jnp.stack([panel, w_rest], 0), mixed)
    second = lax.ppermute(send, "col", [(0, 1), (1, 0)])
    far = jnp.where(is_panel, panel, second[0])
    third = lax.ppermute(far, "row", [(r, r ^ 1) for r in range(16)])
    pick = jnp.stack([is_panel, core == 1, is_panel]).astype(jnp.int32)
    return (pick, second, send, far, third, w_mine, second[1, :16]), later


def spread_general(jacobian, weights, row, col, rows, cols):
    per_dev, samples, width = jacobian.shape
    slabs = weights.shape[0]
    holds = (row == rows - 1) & (col == cols - 1)
    panel = lax.psum(
        jnp.where(holds, jacobian[per_dev - 1], jnp.zeros_like(jacobian[0])), ("row", "col")
    )
    w_panel = lax.psum(
        jnp.where(col == cols - 1, weights[:, -1], jnp.zeros_like(weights[:, 0])), "col"
    )
    slab = jnp.zeros((slabs, samples, width), BF16)
    for offset in range(0, per_dev, slabs):
        piece = lax.slice_in_dim(jacobian, offset, offset + slabs, axis=0)
        pairs = []
        for t in range(rows):
            if (t * slabs) % per_dev == offset:
                home = (t * slabs) // per_dev
                source, target = (home % rows) * cols + home // rows, t * cols
                if source == target:
                    slab = slab + jnp.where((row == t) & (col == 0), piece, jnp.zeros_like(piece))
                else:
                    pairs.append((source, target))
        if pairs:
            slab = slab + lax.ppermute(piece, ("row", "col"), pairs)
    spread = slab
    for c in range(1, cols):
        spread = spread + lax.ppermute(slab, "col", [(0, c)])
    lanes = samples // width
    w_panel = w_panel.reshape(slabs * lanes, width)
    w_panel = jnp.pad(w_panel, ((0, -w_panel.shape[0] % 16), (0, 0)))
    return (jnp.ones((3,), jnp.int32), spread, spread, panel, panel, w_panel, w_panel)


def shards(jacobian, weights, panel_weights, damping, panel_inverse):
    per_dev, samples, width = jacobian.shape
    slabs, col_block, _ = weights.shape
    rows = lax.axis_size("row")
    cols = lax.axis_size("col")
    row = lax.axis_index("row")
    col = lax.axis_index("col")
    panel_id = col_block * cols - 1

    chips = rows // 2
    cycle = chip_cycle(chips, cols)
    place = {c: p for p, c in enumerate(cycle)}
    ring = [(2 * c, 2 * cycle[(place[c] + 1) % chips]) for c in cycle]
    ring += [(2 * c + 1, 2 * cycle[(place[c] - 1) % chips] + 1) for c in cycle]
    swap = [(r, r ^ 1) for r in range(rows)]
    half = per_dev // 2

    def over(value, perm):
        return lax.ppermute(value, "row", perm)

    tail = panel_weights.reshape(2, half, samples // width, width).swapaxes(1, 2)
    tail = tail.reshape(2, per_dev, width)
    tail = jnp.pad(tail, ((0, 0), (0, -per_dev % 16), (0, 0))).reshape(-1, width)
    own = jnp.concatenate([jacobian.reshape(per_dev * samples, width), tail], 0)
    other_core = over(own, swap)
    if (rows, cols, per_dev) == (16, 2, 8 * slabs):
        small, other_core = spread_direct(jacobian, weights, row, col, other_core)
    else:
        small = spread_general(jacobian, weights, row, col, rows, cols)
    hops = [over(own, ring), over(other_core, ring)]
    turned, factor = prep_call(*small, panel_inverse)
    w32 = weights.astype(F32)

    far = chips // 2
    order = [None] + [(d, s) for d in range(1, far) for s in (0, 1)] + [(far, 0)]
    table = np.zeros((rows, len(order), 2, 2), np.int32)
    for r in range(rows):
        p, c = place[r // 2], r % 2
        for n, hop in enumerate(order):
            if hop is None:
                owners = (r, r ^ 1)
            else:
                d, s = hop
                step = d if c else -d
                owners = (
                    2 * cycle[(p + step) % chips] + (c ^ s),
                    2 * cycle[(p - step) % chips] + (1 ^ c ^ s),
                )
            for u, owner in enumerate(owners):
                table[r, n, u] = owner * per_dev + np.array([0, half])
    table = table.reshape(rows, -1)
    starts = lax.dynamic_index_in_dim(jnp.asarray(table), row, 0, keepdims=False)
    base = col * col_block
    ids = row * slabs + jnp.arange(slabs, dtype=jnp.int32) - base
    held = ((ids >= 0) & (ids < col_block)).astype(jnp.int32)
    spots = jnp.stack([jnp.clip(ids, 0, col_block - 1), held], 1).reshape(-1)
    sc = jnp.concatenate([starts, (panel_id - base)[None].astype(jnp.int32), ids])
    sc, spots = lax.optimization_barrier((sc, spots))

    tokens, after = [], []
    gram = jnp.zeros((width, slabs * width), F32)
    shape = (slabs * width, col_block * width)
    out = None

    def compute(units):
        nonlocal out, gram
        out, gram, token = block_call(
            4 * len(tokens), half, sc, units, w32, turned, factor, gram, tuple(after), out, shape
        )
        after.clear()
        tokens.append(token)

    for q in range(len(order) - 1):
        x = hops[q]
        if q == 0:
            x, factor = lax.optimization_barrier((x, factor))
            compute([own, other_core])
        else:
            x, ready = lax.optimization_barrier((x, tokens[q - 1 if q < len(order) - 2 else q]))
            after.append(ready)
        if q + 2 < len(order) - 1:
            hops.append(over(x, ring))
        compute([x, over(x, swap)])
    if cols == 2:
        other = lax.ppermute(gram, "col", [(0, 1), (1, 0)])
    else:
        other = lax.psum(gram, "col") - gram
    return patch_call(spots, gram, other, damping, out)


def solution(mesh):
    return jax.shard_map(
        shards,
        mesh=mesh,
        in_specs=(
            P(("col", "row"), None, None),
            P("row", "col", None),
            P(("col", "row"), None),
            P("row", None),
            P(),
        ),
        out_specs=P("row", "col"),
        check_vma=False,
    )
```

```python
import functools

import jax
import jax.numpy as jnp
import numpy as np
from jax import lax
from jax.experimental import pallas as pl
from jax.experimental.pallas import tpu as pltpu
from jax.sharding import PartitionSpec as P

HIGHEST = lax.Precision.HIGHEST
F32 = jnp.float32
BF16 = jnp.bfloat16


def dot_nt(a, b):
    return lax.dot_general(a, b, (((1,), (1,)), ((), ())), preferred_element_type=F32)


def prep_kernel(pick, slab_a, slab_b, panel_a, panel_b, w_a, w_b, inverse, *outs):
    turned, fac = outs
    slabs, rows, width = slab_a.shape
    lanes = rows // width
    panel = jnp.where(pick[1] > 0, panel_a[...], panel_b[...])
    w = jnp.where(pick[2] > 0, w_a[...], w_b[...]).astype(F32)
    p_t = panel.T
    turned[slabs] = p_t
    for i in range(slabs):
        s = jnp.where(pick[0] > 0, slab_a[i], slab_b[i])
        turned[i] = s.T
        row = jnp.concatenate([w[i * lanes + n : i * lanes + n + 1] for n in range(lanes)], 1)
        scaled = p_t * row.astype(BF16)
        hess = jnp.dot(scaled, s, preferred_element_type=F32)
        fac[i * width : (i + 1) * width] = jnp.dot(
            hess, inverse[...], precision=HIGHEST, preferred_element_type=F32
        )


def prep_call(pick, slab_a, slab_b, panel_a, panel_b, w_a, w_b, inverse):
    slabs, rows, width = slab_a.shape
    return pl.pallas_call(
        prep_kernel,
        in_specs=[pl.BlockSpec(memory_space=pltpu.SMEM)]
        + [pl.BlockSpec(memory_space=pltpu.VMEM)] * 7,
        out_specs=[pl.BlockSpec(memory_space=pltpu.VMEM)] * 2,
        out_shape=[
            jax.ShapeDtypeStruct((slabs + 1, width, rows), BF16),
            jax.ShapeDtypeStruct((slabs * width, width), F32),
        ],
        compiler_params=pltpu.CompilerParams(vmem_limit_bytes=8 << 20),
    )(pick, slab_a, slab_b, panel_a, panel_b, w_a, w_b, inverse)


def block_kernel(slot, half, shape, do_gram, do_rest, count, skip, sc, w, *refs):
    slabs, width, rows = shape
    refs = list(refs)
    if do_rest:
        turned, fac = refs.pop(0), refs.pop(0)
    if do_gram:
        gin = refs.pop(0)
    units, refs = refs[: count // 2], refs[count // 2 + skip :]
    if do_rest:
        out = refs.pop(0)
    if do_gram:
        gout = refs.pop(0)
    token, jbuf, in_sem = refs[:3]
    if do_rest:
        pbuf, obuf, tail_sem, out_sem = refs[3:]
    extra = sc.shape[0] - slabs - 1
    size = half * rows

    def fetch(b):
        unit, h = units[b // 2], b % 2
        copies = [pltpu.make_async_copy(unit.at[pl.ds(h * size, size)], jbuf.at[b], in_sem.at[b])]
        if do_rest:
            tail = pbuf.shape[1]
            at = pl.ds(2 * size + h * tail, tail)
            copies.append(pltpu.make_async_copy(unit.at[at], pbuf.at[b], tail_sem.at[b]))
        return copies

    for b in range(count):
        for copy in fetch(b):
            copy.start()
    token[...] = jnp.zeros_like(token)
    if do_gram:
        gout[...] = gin[...]
    if do_rest:
        fac_b = fac[...].astype(BF16)

    def write(b):
        col = pl.multiple_of(sc[slot + b] * width, half * width)
        return pltpu.make_async_copy(
            obuf.at[b % 2], out.at[:, pl.ds(col, half * width)], out_sem.at[b % 2]
        )

    def one(b, carry):
        pltpu.make_async_copy(units[0].at[pl.ds(0, size)], jbuf.at[b], in_sem.at[b]).wait()
        if do_rest:
            tail = pbuf.shape[1]
            pltpu.make_async_copy(units[0].at[pl.ds(0, tail)], pbuf.at[b], tail_sem.at[b]).wait()

            @pl.when(b >= 2)
            def _():
                write(b - 2).wait()

            pw = pbuf[b].astype(F32)
        first = sc[slot + b]
        acc = None
        parts, panels = [], []
        for k in range(half):
            j = first + k
            jac_t = jbuf[b, k * rows : (k + 1) * rows, :].T
            ws = [
                jnp.where(j == sc[extra + 1 + i], 0.0, w[i, pl.ds(j, 1), :]).astype(BF16)
                for i in range(slabs)
            ]
            if do_rest:
                row_p = jnp.concatenate([pw[k : k + 1], pw[half + k : half + k + 1]], 1)
                row_p = row_p.astype(BF16)
                parts.append(
                    dot_nt(jac_t, jnp.concatenate([turned[i] * ws[i] for i in range(slabs)], 0))
                )
                panels.append(dot_nt(jac_t, turned[slabs] * row_p).astype(BF16))
            if do_gram:
                part = dot_nt(jac_t, jnp.concatenate([jac_t * ws[i] for i in range(slabs)], 0))
                acc = part if acc is None else acc + part
        if do_gram:
            gout[...] += acc
        if do_rest:
            corr = jnp.dot(fac_b, jnp.concatenate(panels, 1), preferred_element_type=F32)
            o = obuf.at[b % 2]
            for k in range(half):
                for i in range(slabs):
                    here = (slice(i * width, (i + 1) * width), slice(k * width, (k + 1) * width))
                    o[here] = parts[k][:, i * width : (i + 1) * width] - corr[here]
            where_p = sc[extra] - first

            @pl.when((where_p >= 0) & (where_p < half))
            def _():
                for k in range(half):

                    @pl.when(where_p == k)
                    def _():
                        o[:, k * width : (k + 1) * width] = fac[...]

            write(b).start()
        return carry

    lax.fori_loop(0, count, one, 0)
    if do_rest:
        for b in range(max(count - 2, 0), count):
            write(b).wait()


def block_call(slot, half, sc, units, w, turned, fac, gram, after, out, shape):
    do_rest, do_gram = turned is not None, gram is not None
    slabs, _, rows = w.shape
    width = units[0].shape[1]
    count = 2 * len(units)
    vmem, anywhere = pl.BlockSpec(memory_space=pltpu.VMEM), pl.BlockSpec(memory_space=pl.ANY)
    args, outs, specs, aliases = [w], [], [], {}
    if do_rest:
        args += [turned, fac]
        outs.append(jax.ShapeDtypeStruct(shape, F32))
        specs.append(anywhere)
    if do_gram:
        aliases[1 + len(args)] = len(outs)
        args.append(gram)
        outs.append(jax.ShapeDtypeStruct(gram.shape, F32))
        specs.append(vmem)
    outs.append(jax.ShapeDtypeStruct((8, 128), F32))
    specs.append(vmem)
    in_specs = [pl.BlockSpec(memory_space=pltpu.SMEM)] + [vmem] * len(args)
    args += list(units) + list(after)
    in_specs += [pl.BlockSpec(memory_space=pltpu.HBM)] * len(units) + [anywhere] * len(after)
    skip = len(after)
    if do_rest and out is not None:
        aliases[1 + len(args)] = 0
        args.append(out)
        in_specs.append(anywhere)
        skip += 1
    stations = half * count
    tail = units[0].shape[0] // 2 - half * rows
    scratch = [
        pltpu.VMEM((count, half * rows, width), BF16),
        pltpu.SemaphoreType.DMA((count,)),
    ]
    if do_rest:
        scratch += [
            pltpu.VMEM((count, tail, width), BF16),
            pltpu.VMEM((2, slabs * width, half * width), F32),
            pltpu.SemaphoreType.DMA((count,)),
            pltpu.SemaphoreType.DMA((2,)),
        ]
    results = pl.pallas_call(
        functools.partial(
            block_kernel, slot, half, (slabs, width, rows), do_gram, do_rest, count, skip
        ),
        in_specs=in_specs,
        out_specs=specs,
        out_shape=outs,
        scratch_shapes=scratch,
        input_output_aliases=aliases,
        compiler_params=pltpu.CompilerParams(vmem_limit_bytes=24 << 20),
        cost_estimate=pl.CostEstimate(
            flops=stations * (4 * do_gram + 10 * do_rest) * width * width * rows // 8,
            bytes_accessed=stations * (do_rest * slabs * width * width * 4 + rows * width * 2) // 8,
            transcendentals=0,
        ),
    )(sc, *args)
    results = list(results)
    out = results.pop(0) if do_rest else out
    gram = results.pop(0) if do_gram else gram
    return out, gram, results[0]


def patch_kernel(sc, gram, other, damp, tile, out):
    i = pl.program_id(0)
    width = tile.shape[0]
    g = (gram[...] + other[...]).T
    eye = lax.broadcasted_iota(jnp.int32, (width, width), 0) == lax.broadcasted_iota(
        jnp.int32, (width, width), 1
    )
    full = jnp.where(eye, g * (1.0 + damp[pl.ds(i, 1), :]), g)
    out[...] = jnp.where(sc[2 * i + 1] > 0, tile[...] + full, tile[...])


def patch_call(sc, gram, other, damping, out):
    slabs, width = damping.shape
    tile = pl.BlockSpec((width, width), lambda i, s: (i, s[2 * i]))
    part = pl.BlockSpec((width, width), lambda i, s: (0, i))
    return pl.pallas_call(
        patch_kernel,
        grid_spec=pltpu.PrefetchScalarGridSpec(
            num_scalar_prefetch=1,
            grid=(slabs,),
            in_specs=[part, part, pl.BlockSpec((slabs, width), lambda i, s: (0, 0)), tile],
            out_specs=tile,
        ),
        out_shape=jax.ShapeDtypeStruct(out.shape, F32),
        input_output_aliases={4: 0},
        compiler_params=pltpu.CompilerParams(vmem_limit_bytes=8 << 20),
    )(sc, gram, other, damping, out)


def chip_cycle(chips, cols):
    if cols == 2:
        return list(range(0, chips, 2)) + list(range(chips - 1, 0, -2))
    half = chips // 2
    return list(range(half)) + list(range(chips - 1, half - 1, -1))


def spread_direct(jacobian, weights, row, col, later):
    per_dev, samples, width = jacobian.shape
    slabs = weights.shape[0]
    core, y = row % 2, (row // 2) % 2
    both = ("row", "col")
    w_mine = weights[:, -1].reshape(slabs * samples // width, width)
    w_mine = jnp.pad(w_mine, ((0, 16 - w_mine.shape[0]), (0, 0)))
    quads = 2 * slabs
    ends = [None, (11, 1), (7, 1), (3, 1)]
    is_panel = col == 1
    mine = jacobian[per_dev - 1]
    panel_pay = jnp.concatenate([mine[None]] + [jnp.zeros_like(jacobian[: quads - 1])], 0)
    total = jnp.where((row == 15) & is_panel, panel_pay, jnp.zeros_like(panel_pay))
    total = total + jnp.where((row == 0) & (col == 0), jacobian[:quads], jnp.zeros_like(panel_pay))
    for m in (1, 2, 3, 0):
        pay = jnp.where(is_panel, panel_pay, lax.slice_in_dim(jacobian, quads * m, quads * (m + 1)))
        pairs = [(2, 2 * (8 + 2 * m))]
        if m:
            pairs += [(0, 4 * m), (31, 2 * ends[m][0] + ends[m][1])]
        total = total + lax.ppermute(pay, both, pairs)
    hop = [(2 * r, 2 * (r ^ 1)) for r in range(16)] + [(2 * r + 1, 2 * (r ^ 2) + 1) for r in range(16)]
    total, later = lax.optimization_barrier((total, later))
    first = lax.ppermute(jnp.where(is_panel, total[:slabs], total[slabs:]), both, hop)
    panel = jnp.where(y == 1, total[0], first[0])
    w_rest = jnp.pad(w_mine, ((0, samples - 16), (0, 0)))
    mixed = jnp.where(core == 0, total[:slabs], first)
    send = jnp.where(is_panel, jnp.stack([panel, w_rest], 0), mixed)
    second = lax.ppermute(send, "col", [(0, 1), (1, 0)])
    far = jnp.where(is_panel, panel, second[0])
    third = lax.ppermute(far, "row", [(r, r ^ 1) for r in range(16)])
    pick = jnp.stack([is_panel, core == 1, is_panel]).astype(jnp.int32)
    return (pick, second, send, far, third, w_mine, second[1, :16]), later


def spread_general(jacobian, weights, row, col, rows, cols):
    per_dev, samples, width = jacobian.shape
    slabs = weights.shape[0]
    holds = (row == rows - 1) & (col == cols - 1)
    panel = lax.psum(
        jnp.where(holds, jacobian[per_dev - 1], jnp.zeros_like(jacobian[0])), ("row", "col")
    )
    w_panel = lax.psum(
        jnp.where(col == cols - 1, weights[:, -1], jnp.zeros_like(weights[:, 0])), "col"
    )
    slab = jnp.zeros((slabs, samples, width), BF16)
    for offset in range(0, per_dev, slabs):
        piece = lax.slice_in_dim(jacobian, offset, offset + slabs, axis=0)
        pairs = []
        for t in range(rows):
            if (t * slabs) % per_dev == offset:
                home = (t * slabs) // per_dev
                source, target = (home % rows) * cols + home // rows, t * cols
                if source == target:
                    slab = slab + jnp.where((row == t) & (col == 0), piece, jnp.zeros_like(piece))
                else:
                    pairs.append((source, target))
        if pairs:
            slab = slab + lax.ppermute(piece, ("row", "col"), pairs)
    spread = slab
    for c in range(1, cols):
        spread = spread + lax.ppermute(slab, "col", [(0, c)])
    lanes = samples // width
    w_panel = w_panel.reshape(slabs * lanes, width)
    w_panel = jnp.pad(w_panel, ((0, -w_panel.shape[0] % 16), (0, 0)))
    return (jnp.ones((3,), jnp.int32), spread, spread, panel, panel, w_panel, w_panel)


def shards(jacobian, weights, panel_weights, damping, panel_inverse):
    per_dev, samples, width = jacobian.shape
    slabs, col_block, _ = weights.shape
    rows = lax.axis_size("row")
    cols = lax.axis_size("col")
    row = lax.axis_index("row")
    col = lax.axis_index("col")
    panel_id = col_block * cols - 1

    chips = rows // 2
    cycle = chip_cycle(chips, cols)
    place = {c: p for p, c in enumerate(cycle)}
    ring = [(2 * c, 2 * cycle[(place[c] + 1) % chips]) for c in cycle]
    ring += [(2 * c + 1, 2 * cycle[(place[c] - 1) % chips] + 1) for c in cycle]
    swap = [(r, r ^ 1) for r in range(rows)]
    half = per_dev // 2

    def over(value, perm):
        return lax.ppermute(value, "row", perm)

    tail = panel_weights.reshape(2, half, samples // width, width).swapaxes(1, 2)
    tail = tail.reshape(2, per_dev, width)
    tail = jnp.pad(tail, ((0, 0), (0, -per_dev % 16), (0, 0))).reshape(-1, width)
    own = jnp.concatenate([jacobian.reshape(per_dev * samples, width), tail], 0)
    w32 = weights.astype(F32)
    far = chips // 2
    order = [None] + [(d, s) for d in range(1, far) for s in (0, 1)] + [(far, 0)]
    table = np.zeros((rows, len(order), 2, 2), np.int32)
    for r in range(rows):
        p, c = place[r // 2], r % 2
        for n, hop in enumerate(order):
            if hop is None:
                owners = (r, r ^ 1)
            else:
                d, s = hop
                step = d if c else -d
                owners = (
                    2 * cycle[(p + step) % chips] + (c ^ s),
                    2 * cycle[(p - step) % chips] + (1 ^ c ^ s),
                )
            for u, owner in enumerate(owners):
                table[r, n, u] = owner * per_dev + np.array([0, half])
    table = table.reshape(rows, -1)
    starts = lax.dynamic_index_in_dim(jnp.asarray(table), row, 0, keepdims=False)
    base = col * col_block
    ids = row * slabs + jnp.arange(slabs, dtype=jnp.int32) - base
    held = ((ids >= 0) & (ids < col_block)).astype(jnp.int32)
    spots = jnp.stack([jnp.clip(ids, 0, col_block - 1), held], 1).reshape(-1)
    sc = jnp.concatenate([starts, (panel_id - base)[None].astype(jnp.int32), ids])
    sc, spots = lax.optimization_barrier((sc, spots))

    after, hops = [], [over(own, ring)]
    gram = jnp.zeros((width, slabs * width), F32)
    shape = (slabs * width, col_block * width)
    out = None

    def compute(slot, units, do_gram=True, do_rest=True):
        nonlocal out, gram
        out, g, token = block_call(
            slot, half, sc, units, w32, turned if do_rest else None, factor if do_rest else None,
            gram if do_gram else None, tuple(after), out, shape,
        )
        gram = g if do_gram else gram
        after.clear()
        return token

    def hold(x, ready):
        x, ready = lax.optimization_barrier((x, ready))
        after.append(ready)
        return x

    other_core = late = over(own, swap)
    if (rows, cols, per_dev) == (16, 2, 8 * slabs):
        small, late = spread_direct(jacobian, weights, row, col, other_core)
    else:
        small = spread_general(jacobian, weights, row, col, rows, cols)
    turned, factor = prep_call(*small, panel_inverse)
    hops[0], factor = lax.optimization_barrier((hops[0], factor))
    hops += [over(late, ring), over(hops[0], ring)]
    last = len(order) - 2
    pending = [hops[0], over(hops[0], swap)]
    token = compute(0, [own, other_core])
    for q in range(1, last + 1):
        if q < last:
            x = hold(hops[q], token)
            if q + 2 <= last:
                hops.append(over(x, ring))
            units = [x, over(x, swap)]
            token = compute(4 * q, pending)
            pending = units
        else:
            token = compute(4 * q, pending)
            x = hold(hops[q], token)
            units = [x, over(x, swap)]
    after.append(compute(4 * last + 4, units, do_rest=False))
    compute(4 * last + 4, units, do_gram=False)
    if cols == 2:
        other = lax.ppermute(gram, "col", [(0, 1), (1, 0)])
    else:
        other = lax.psum(gram, "col") - gram
    return patch_call(spots, gram, other, damping, out)


def solution(mesh):
    return jax.shard_map(
        shards,
        mesh=mesh,
        in_specs=(
            P(("col", "row"), None, None),
            P("row", "col", None),
            P(("col", "row"), None),
            P("row", None),
            P(),
        ),
        out_specs=P("row", "col"),
        check_vma=False,
    )
```

```python
import functools

import jax
import jax.numpy as jnp
import numpy as np
from jax import lax
from jax.experimental import pallas as pl
from jax.experimental.pallas import tpu as pltpu
from jax.sharding import PartitionSpec as P

HIGHEST = lax.Precision.HIGHEST
F32 = jnp.float32
BF16 = jnp.bfloat16


def dot_nt(a, b):
    return lax.dot_general(a, b, (((1,), (1,)), ((), ())), preferred_element_type=F32)


def prep_kernel(pick, slab_a, slab_b, panel_a, panel_b, w_a, w_b, inverse, *outs):
    turned, fac = outs
    slabs, rows, width = slab_a.shape
    lanes = rows // width
    panel = jnp.where(pick[1] > 0, panel_a[...], panel_b[...])
    w = jnp.where(pick[2] > 0, w_a[...], w_b[...]).astype(F32)
    p_t = panel.T
    turned[slabs] = p_t
    for i in range(slabs):
        s = jnp.where(pick[0] > 0, slab_a[i], slab_b[i])
        turned[i] = s.T
        row = jnp.concatenate([w[i * lanes + n : i * lanes + n + 1] for n in range(lanes)], 1)
        scaled = p_t * row.astype(BF16)
        hess = jnp.dot(scaled, s, preferred_element_type=F32)
        fac[i * width : (i + 1) * width] = jnp.dot(
            hess, inverse[...], precision=HIGHEST, preferred_element_type=F32
        )


def prep_call(pick, slab_a, slab_b, panel_a, panel_b, w_a, w_b, inverse):
    slabs, rows, width = slab_a.shape
    return pl.pallas_call(
        prep_kernel,
        in_specs=[pl.BlockSpec(memory_space=pltpu.SMEM)]
        + [pl.BlockSpec(memory_space=pltpu.VMEM)] * 7,
        out_specs=[pl.BlockSpec(memory_space=pltpu.VMEM)] * 2,
        out_shape=[
            jax.ShapeDtypeStruct((slabs + 1, width, rows), BF16),
            jax.ShapeDtypeStruct((slabs * width, width), F32),
        ],
        compiler_params=pltpu.CompilerParams(vmem_limit_bytes=8 << 20),
    )(pick, slab_a, slab_b, panel_a, panel_b, w_a, w_b, inverse)


def block_kernel(slot, half, shape, do_gram, do_rest, count, skip, sc, w, *refs):
    slabs, width, rows = shape
    refs = list(refs)
    if do_rest:
        turned, fac = refs.pop(0), refs.pop(0)
    if do_gram:
        gin = refs.pop(0)
    units, refs = refs[: count // 2], refs[count // 2 + skip :]
    if do_rest:
        out = refs.pop(0)
    if do_gram:
        gout = refs.pop(0)
    token, jbuf, in_sem = refs[:3]
    if do_rest:
        pbuf, obuf, tail_sem, out_sem = refs[3:]
    extra = sc.shape[0] - slabs - 1
    size = half * rows

    def fetch(b):
        unit, h = units[b // 2], b % 2
        copies = [pltpu.make_async_copy(unit.at[pl.ds(h * size, size)], jbuf.at[b], in_sem.at[b])]
        if do_rest:
            tail = pbuf.shape[1]
            at = pl.ds(2 * size + h * tail, tail)
            copies.append(pltpu.make_async_copy(unit.at[at], pbuf.at[b], tail_sem.at[b]))
        return copies

    for b in range(count):
        for copy in fetch(b):
            copy.start()
    token[...] = jnp.zeros_like(token)
    if do_gram:
        gout[...] = gin[...]
    if do_rest:
        fac_b = fac[...].astype(BF16)

    def write(b):
        col = pl.multiple_of(sc[slot + b] * width, half * width)
        return pltpu.make_async_copy(
            obuf.at[b % 2], out.at[:, pl.ds(col, half * width)], out_sem.at[b % 2]
        )

    def one(b, carry):
        pltpu.make_async_copy(units[0].at[pl.ds(0, size)], jbuf.at[b], in_sem.at[b]).wait()
        if do_rest:
            tail = pbuf.shape[1]
            pltpu.make_async_copy(units[0].at[pl.ds(0, tail)], pbuf.at[b], tail_sem.at[b]).wait()

            @pl.when(b >= 2)
            def _():
                write(b - 2).wait()

            pw = pbuf[b].astype(F32)
        first = sc[slot + b]
        acc = None
        parts, panels = [], []
        for k in range(half):
            j = first + k
            jac_t = jbuf[b, k * rows : (k + 1) * rows, :].T
            ws = [
                jnp.where(j == sc[extra + 1 + i], 0.0, w[i, pl.ds(j, 1), :]).astype(BF16)
                for i in range(slabs)
            ]
            if do_rest:
                row_p = jnp.concatenate([pw[k : k + 1], pw[half + k : half + k + 1]], 1)
                row_p = row_p.astype(BF16)
                parts.append(
                    dot_nt(jac_t, jnp.concatenate([turned[i] * ws[i] for i in range(slabs)], 0))
                )
                panels.append(dot_nt(jac_t, turned[slabs] * row_p).astype(BF16))
            if do_gram:
                part = dot_nt(jac_t, jnp.concatenate([jac_t * ws[i] for i in range(slabs)], 0))
                acc = part if acc is None else acc + part
        if do_gram:
            gout[...] += acc
        if do_rest:
            corr = jnp.dot(fac_b, jnp.concatenate(panels, 1), preferred_element_type=F32)
            o = obuf.at[b % 2]
            for k in range(half):
                for i in range(slabs):
                    here = (slice(i * width, (i + 1) * width), slice(k * width, (k + 1) * width))
                    o[here] = parts[k][:, i * width : (i + 1) * width] - corr[here]
            where_p = sc[extra] - first

            @pl.when((where_p >= 0) & (where_p < half))
            def _():
                for k in range(half):

                    @pl.when(where_p == k)
                    def _():
                        o[:, k * width : (k + 1) * width] = fac[...]

            write(b).start()
        return carry

    lax.fori_loop(0, count, one, 0)
    if do_rest:
        for b in range(max(count - 2, 0), count):
            write(b).wait()


def block_call(slot, half, sc, units, w, turned, fac, gram, after, out, shape):
    do_rest, do_gram = turned is not None, gram is not None
    slabs, _, rows = w.shape
    width = units[0].shape[1]
    count = 2 * len(units)
    vmem, anywhere = pl.BlockSpec(memory_space=pltpu.VMEM), pl.BlockSpec(memory_space=pl.ANY)
    args, outs, specs, aliases = [w], [], [], {}
    if do_rest:
        args += [turned, fac]
        outs.append(jax.ShapeDtypeStruct(shape, F32))
        specs.append(anywhere)
    if do_gram:
        aliases[1 + len(args)] = len(outs)
        args.append(gram)
        outs.append(jax.ShapeDtypeStruct(gram.shape, F32))
        specs.append(vmem)
    outs.append(jax.ShapeDtypeStruct((8, 128), F32))
    specs.append(vmem)
    in_specs = [pl.BlockSpec(memory_space=pltpu.SMEM)] + [vmem] * len(args)
    args += list(units) + list(after)
    in_specs += [pl.BlockSpec(memory_space=pltpu.HBM)] * len(units) + [anywhere] * len(after)
    skip = len(after)
    if do_rest and out is not None:
        aliases[1 + len(args)] = 0
        args.append(out)
        in_specs.append(anywhere)
        skip += 1
    stations = half * count
    tail = units[0].shape[0] // 2 - half * rows
    scratch = [
        pltpu.VMEM((count, half * rows, width), BF16),
        pltpu.SemaphoreType.DMA((count,)),
    ]
    if do_rest:
        scratch += [
            pltpu.VMEM((count, tail, width), BF16),
            pltpu.VMEM((2, slabs * width, half * width), F32),
            pltpu.SemaphoreType.DMA((count,)),
            pltpu.SemaphoreType.DMA((2,)),
        ]
    results = pl.pallas_call(
        functools.partial(
            block_kernel, slot, half, (slabs, width, rows), do_gram, do_rest, count, skip
        ),
        in_specs=in_specs,
        out_specs=specs,
        out_shape=outs,
        scratch_shapes=scratch,
        input_output_aliases=aliases,
        compiler_params=pltpu.CompilerParams(vmem_limit_bytes=24 << 20),
        cost_estimate=pl.CostEstimate(
            flops=stations * (4 * do_gram + 10 * do_rest) * width * width * rows // 8,
            bytes_accessed=stations * (do_rest * slabs * width * width * 4 + rows * width * 2) // 8,
            transcendentals=0,
        ),
    )(sc, *args)
    results = list(results)
    out = results.pop(0) if do_rest else out
    gram = results.pop(0) if do_gram else gram
    return out, gram, results[0]


def patch_kernel(sc, gram, other, damp, tiles, out, buf, in_sem, out_sem):
    slabs, width, _ = buf.shape

    def spot(ref, i):
        col = pl.multiple_of(sc[2 * i] * width, width)
        return ref.at[pl.ds(i * width, width), pl.ds(col, width)]

    reads = [pltpu.make_async_copy(spot(tiles, i), buf.at[i], in_sem.at[i]) for i in range(slabs)]
    writes = [pltpu.make_async_copy(buf.at[i], spot(out, i), out_sem.at[i]) for i in range(slabs)]
    for copy in reads:
        copy.start()
    eye = lax.broadcasted_iota(jnp.int32, (width, width), 0) == lax.broadcasted_iota(
        jnp.int32, (width, width), 1
    )
    for i in range(slabs):
        here = (slice(None), slice(i * width, (i + 1) * width))
        g = (gram[here] + other[here]).T
        full = jnp.where(eye, g * (1.0 + damp[i : i + 1, :]), g)
        reads[i].wait()
        buf[i] = jnp.where(sc[2 * i + 1] > 0, buf[i] + full, buf[i])
        writes[i].start()
    for copy in writes:
        copy.wait()


def patch_call(sc, gram, other, damping, out):
    slabs, width = damping.shape
    vmem, anywhere = pl.BlockSpec(memory_space=pltpu.VMEM), pl.BlockSpec(memory_space=pl.ANY)
    return pl.pallas_call(
        patch_kernel,
        in_specs=[pl.BlockSpec(memory_space=pltpu.SMEM), vmem, vmem, vmem, anywhere],
        out_specs=anywhere,
        out_shape=jax.ShapeDtypeStruct(out.shape, F32),
        scratch_shapes=[
            pltpu.VMEM((slabs, width, width), F32),
            pltpu.SemaphoreType.DMA((slabs,)),
            pltpu.SemaphoreType.DMA((slabs,)),
        ],
        input_output_aliases={4: 0},
        compiler_params=pltpu.CompilerParams(vmem_limit_bytes=8 << 20),
    )(sc, gram, other, damping, out)


def chip_cycle(chips, cols):
    if cols == 2:
        return list(range(0, chips, 2)) + list(range(chips - 1, 0, -2))
    half = chips // 2
    return list(range(half)) + list(range(chips - 1, half - 1, -1))


def spread_direct(jacobian, weights, row, col, later):
    per_dev, samples, width = jacobian.shape
    slabs = weights.shape[0]
    core, y = row % 2, (row // 2) % 2
    both = ("row", "col")
    w_mine = weights[:, -1].reshape(slabs * samples // width, width)
    w_mine = jnp.pad(w_mine, ((0, 16 - w_mine.shape[0]), (0, 0)))
    quads = 2 * slabs
    ends = [None, (11, 1), (7, 1), (3, 1)]
    is_panel = col == 1
    mine = jacobian[per_dev - 1]
    panel_pay = jnp.concatenate([mine[None]] + [jnp.zeros_like(jacobian[: quads - 1])], 0)
    total = jnp.where((row == 15) & is_panel, panel_pay, jnp.zeros_like(panel_pay))
    total = total + jnp.where((row == 0) & (col == 0), jacobian[:quads], jnp.zeros_like(panel_pay))
    for m in (1, 2, 3, 0):
        pay = jnp.where(is_panel, panel_pay, lax.slice_in_dim(jacobian, quads * m, quads * (m + 1)))
        pairs = [(2, 2 * (8 + 2 * m))]
        if m:
            pairs += [(0, 4 * m), (31, 2 * ends[m][0] + ends[m][1])]
        total = total + lax.ppermute(pay, both, pairs)
    hop = [(2 * r, 2 * (r ^ 1)) for r in range(16)] + [(2 * r + 1, 2 * (r ^ 2) + 1) for r in range(16)]
    total, later = lax.optimization_barrier((total, later))
    first = lax.ppermute(jnp.where(is_panel, total[:slabs], total[slabs:]), both, hop)
    panel = jnp.where(y == 1, total[0], first[0])
    w_rest = jnp.pad(w_mine, ((0, samples - 16), (0, 0)))
    mixed = jnp.where(core == 0, total[:slabs], first)
    send = jnp.where(is_panel, jnp.stack([panel, w_rest], 0), mixed)
    second = lax.ppermute(send, "col", [(0, 1), (1, 0)])
    far = jnp.where(is_panel, panel, second[0])
    third = lax.ppermute(far, "row", [(r, r ^ 1) for r in range(16)])
    pick = jnp.stack([is_panel, core == 1, is_panel]).astype(jnp.int32)
    return (pick, second, send, far, third, w_mine, second[1, :16]), later


def spread_general(jacobian, weights, row, col, rows, cols):
    per_dev, samples, width = jacobian.shape
    slabs = weights.shape[0]
    holds = (row == rows - 1) & (col == cols - 1)
    panel = lax.psum(
        jnp.where(holds, jacobian[per_dev - 1], jnp.zeros_like(jacobian[0])), ("row", "col")
    )
    w_panel = lax.psum(
        jnp.where(col == cols - 1, weights[:, -1], jnp.zeros_like(weights[:, 0])), "col"
    )
    slab = jnp.zeros((slabs, samples, width), BF16)
    for offset in range(0, per_dev, slabs):
        piece = lax.slice_in_dim(jacobian, offset, offset + slabs, axis=0)
        pairs = []
        for t in range(rows):
            if (t * slabs) % per_dev == offset:
                home = (t * slabs) // per_dev
                source, target = (home % rows) * cols + home // rows, t * cols
                if source == target:
                    slab = slab + jnp.where((row == t) & (col == 0), piece, jnp.zeros_like(piece))
                else:
                    pairs.append((source, target))
        if pairs:
            slab = slab + lax.ppermute(piece, ("row", "col"), pairs)
    spread = slab
    for c in range(1, cols):
        spread = spread + lax.ppermute(slab, "col", [(0, c)])
    lanes = samples // width
    w_panel = w_panel.reshape(slabs * lanes, width)
    w_panel = jnp.pad(w_panel, ((0, -w_panel.shape[0] % 16), (0, 0)))
    return (jnp.ones((3,), jnp.int32), spread, spread, panel, panel, w_panel, w_panel)


def shards(jacobian, weights, panel_weights, damping, panel_inverse):
    per_dev, samples, width = jacobian.shape
    slabs, col_block, _ = weights.shape
    rows = lax.axis_size("row")
    cols = lax.axis_size("col")
    row = lax.axis_index("row")
    col = lax.axis_index("col")
    panel_id = col_block * cols - 1

    chips = rows // 2
    cycle = chip_cycle(chips, cols)
    place = {c: p for p, c in enumerate(cycle)}
    ring = [(2 * c, 2 * cycle[(place[c] + 1) % chips]) for c in cycle]
    ring += [(2 * c + 1, 2 * cycle[(place[c] - 1) % chips] + 1) for c in cycle]
    swap = [(r, r ^ 1) for r in range(rows)]
    half = per_dev // 2

    def over(value, perm):
        return lax.ppermute(value, "row", perm)

    tail = panel_weights.reshape(2, half, samples // width, width).swapaxes(1, 2)
    tail = tail.reshape(2, per_dev, width)
    tail = jnp.pad(tail, ((0, 0), (0, -per_dev % 16), (0, 0))).reshape(-1, width)
    own = jnp.concatenate([jacobian.reshape(per_dev * samples, width), tail], 0)
    w32 = weights.astype(F32)
    far = chips // 2
    order = [None] + [(d, s) for d in range(1, far) for s in (0, 1)] + [(far, 0)]
    table = np.zeros((rows, len(order), 2, 2), np.int32)
    for r in range(rows):
        p, c = place[r // 2], r % 2
        for n, hop in enumerate(order):
            if hop is None:
                owners = (r, r ^ 1)
            else:
                d, s = hop
                step = d if c else -d
                owners = (
                    2 * cycle[(p + step) % chips] + (c ^ s),
                    2 * cycle[(p - step) % chips] + (1 ^ c ^ s),
                )
            for u, owner in enumerate(owners):
                table[r, n, u] = owner * per_dev + np.array([0, half])
    table = table.reshape(rows, -1)
    starts = lax.dynamic_index_in_dim(jnp.asarray(table), row, 0, keepdims=False)
    base = col * col_block
    ids = row * slabs + jnp.arange(slabs, dtype=jnp.int32) - base
    held = ((ids >= 0) & (ids < col_block)).astype(jnp.int32)
    spots = jnp.stack([jnp.clip(ids, 0, col_block - 1), held], 1).reshape(-1)
    sc = jnp.concatenate([starts, (panel_id - base)[None].astype(jnp.int32), ids])
    sc, spots = lax.optimization_barrier((sc, spots))

    after, hops = [], [over(own, ring)]
    gram = jnp.zeros((width, slabs * width), F32)
    shape = (slabs * width, col_block * width)
    out = None

    def compute(slot, units, do_gram=True, do_rest=True):
        nonlocal out, gram
        out, g, token = block_call(
            slot, half, sc, units, w32, turned if do_rest else None, factor if do_rest else None,
            gram if do_gram else None, tuple(after), out, shape,
        )
        gram = g if do_gram else gram
        after.clear()
        return token

    def hold(x, ready):
        x, ready = lax.optimization_barrier((x, ready))
        after.append(ready)
        return x

    other_core = late = over(own, swap)
    if (rows, cols, per_dev) == (16, 2, 8 * slabs):
        small, late = spread_direct(jacobian, weights, row, col, other_core)
    else:
        small = spread_general(jacobian, weights, row, col, rows, cols)
    turned, factor = prep_call(*small, panel_inverse)
    hops[0], factor = lax.optimization_barrier((hops[0], factor))
    hops += [over(late, ring), over(hops[0], ring)]
    last = len(order) - 2
    pending = [hops[0], over(hops[0], swap)]
    token = compute(0, [own, other_core])
    for q in range(1, last + 1):
        if q < last:
            x = hold(hops[q], token)
            if q + 2 <= last:
                hops.append(over(x, ring))
            units = [x, over(x, swap)]
            token = compute(4 * q, pending)
            pending = units
        else:
            token = compute(4 * q, pending)
            x = hold(hops[q], token)
            units = [x, over(x, swap)]
    after.append(compute(4 * last + 4, units, do_rest=False))
    compute(4 * last + 4, units, do_gram=False)
    if cols == 2:
        other = lax.ppermute(gram, "col", [(0, 1), (1, 0)])
    else:
        other = lax.psum(gram, "col") - gram
    return patch_call(spots, gram, other, damping, out)


def solution(mesh):
    return jax.shard_map(
        shards,
        mesh=mesh,
        in_specs=(
            P(("col", "row"), None, None),
            P("row", "col", None),
            P(("col", "row"), None),
            P("row", None),
            P(),
        ),
        out_specs=P("row", "col"),
        check_vma=False,
    )
```
